32 devices in a mesh: seqs: 4 (over y, x), blk: 4 (over z), mp: 2 (over core).
Axes of the slice: x: 2, y: 2, z: 4, core: 2. Of those that a mesh axis runs over, the one named last changes fastest.
Arguments:
- block_input: float32 [2048, 1536], P(('seqs', 'blk')), may hold values from -6 to 6
- cotangent: float32 [2048, 1536], P(('seqs', 'blk')), may hold values from -6 to 6
- lengths: int32 [4], P('seqs'), may hold values from 128 to 512, as said below
- offsets: int32 [4], P('seqs'), may hold values from 2048 to 4095
- ssm_state: bfloat16 [4, 16, 3072], P('seqs', None, ('blk', 'mp')), may hold values from -6 to 6
- conv_state: bfloat16 [4, 3, 3072], P('seqs', None, ('blk', 'mp')), may hold values from -6 to 6
- kv_cache: bfloat16 [4, 2, 2048, 1536], P('seqs', None, 'blk', 'mp'), may hold values from -6 to 6
- norm_gains: bfloat16 [4, 1536], P(None, 'blk'), may hold values from 0.5 to 1.5
- w_in: bfloat16 [2, 1536, 3072], P(None, None, ('blk', 'mp')), may hold values from -0.15625 to 0.15625
- conv_weight: bfloat16 [4, 3072], P(None, ('blk', 'mp')), may hold values from -3 to 3
- conv_bias: bfloat16 [3072], P(('blk', 'mp')), may hold values from -3 to 3
- x_proj: bfloat16 [128, 3072], P(None, ('blk', 'mp')), may hold values from -0.109375 to 0.109375
- dt_proj: bfloat16 [96, 3072], P(None, ('blk', 'mp')), may hold values from -0.625 to 0.625
- dt_bias: bfloat16 [3072], P(('blk', 'mp')), may hold values from -5 to -3
- a_log: bfloat16 [16, 3072], P(None, ('blk', 'mp'))
- d_skip: bfloat16 [3072], P(('blk', 'mp')), may hold values from 0.5 to 1.5
- mamba_out: bfloat16 [3072, 1536], P(('blk', 'mp')), may hold values from -0.109375 to 0.109375
- ffn1_gate_up: bfloat16 [2, 1536, 4096], P(None, None, ('blk', 'mp')), may hold values from -0.15625 to 0.15625
- ffn1_down: bfloat16 [4096, 1536], P(('blk', 'mp')), may hold values from -0.09375 to 0.09375
- qkv_proj: bfloat16 [3, 1536, 1536], P(None, 'blk', 'mp'), may hold values from -0.15625 to 0.15625
- attn_out: bfloat16 [1536, 1536], P('mp', 'blk'), may hold values from -3.5 to 3.5
- ffn2_gate_up: bfloat16 [2, 1536, 4096], P(None, None, ('blk', 'mp')), may hold values from -0.15625 to 0.15625
- ffn2_down: bfloat16 [4096, 1536], P(('blk', 'mp')), may hold values from -0.09375 to 0.09375
Outputs:
- block_output: float32 [2048, 1536], P(('seqs', 'blk'))
- input_grad: float32 [2048, 1536], P(('seqs', 'blk'))
- new_ssm_state: bfloat16 [4, 16, 3072], P('seqs', None, ('blk', 'mp'))
- new_conv_state: bfloat16 [4, 3, 3072], P('seqs', None, ('blk', 'mp'))
- new_kv_cache: bfloat16 [4, 2, 2048, 1536], P('seqs', None, 'blk', 'mp')
- ssm_state_grad: float32 [4, 16, 3072], P('seqs', None, ('blk', 'mp'))
- conv_state_grad: float32 [4, 3, 3072], P('seqs', None, ('blk', 'mp'))
- kv_cache_grad: float32 [4, 2, 2048, 1536], P('seqs', None, 'blk', 'mp')
- norm_gains_grad: float32 [4, 1536], P(None, 'blk')
- w_in_grad: float32 [2, 1536, 3072], P(None, None, ('blk', 'mp'))
- conv_weight_grad: float32 [4, 3072], P(None, ('blk', 'mp'))
- conv_bias_grad: float32 [3072], P(('blk', 'mp'))
- x_proj_grad: float32 [128, 3072], P(None, ('blk', 'mp'))
- dt_proj_grad: float32 [96, 3072], P(None, ('blk', 'mp'))
- dt_bias_grad: float32 [3072], P(('blk', 'mp'))
- a_log_grad: float32 [16, 3072], P(None, ('blk', 'mp'))
- d_skip_grad: float32 [3072], P(('blk', 'mp'))
- mamba_out_grad: float32 [3072, 1536], P(('blk', 'mp'))
- ffn1_gate_up_grad: float32 [2, 1536, 4096], P(None, None, ('blk', 'mp'))
- ffn1_down_grad: float32 [4096, 1536], P(('blk', 'mp'))
- qkv_proj_grad: float32 [3, 1536, 1536], P(None, 'blk', 'mp')
- attn_out_grad: float32 [1536, 1536], P('mp', 'blk')
- ffn2_gate_up_grad: float32 [2, 1536, 4096], P(None, None, ('blk', 'mp'))
- ffn2_down_grad: float32 [4096, 1536], P(('blk', 'mp'))
The draws below stay inside these ranges and needn't reach their ends.
Inputs may be any that keep to these rules, and one draw needn't show every extreme that they name: `lengths`: one sequence has exactly 512 tokens and one exactly 128; the others lie between.
All inputs are finite; a program needn't handle non-finite values.
Results may differ from the reference program's by a relative error of at most 0.039.
Values may be sent and summed in bfloat16 or wider, within the bound.
No kernel may reach another device: no remote copies, remote signals or barrier semaphores. Data moves between devices by JAX's collectives and lax.ppermute only.
A program may use at most 512 MiB of HBM per device.

```python
import jax
import jax.numpy as jnp
from jax import lax

D = 1536
DI = 3072
NS = 16
KC = 4
R = 96
FF = 4096
H = 12
HD = 128
W = 2048
P_SIZE = 128
TOK_DEV = 128
LEN = 512
ROWS = 2048
N_SEQS = 4


def draw_lengths(key, part):
    key_pick, key_order = jax.random.split(key)
    middle = jax.random.randint(key_pick, (N_SEQS,), LEN // 4, LEN + 1)
    shuffle = jax.random.permutation(key_order, N_SEQS)
    middle = jnp.where(shuffle == 0, LEN, middle)
    middle = jnp.where(shuffle == 1, LEN // 4, middle)
    return middle.astype(jnp.int32)


def draw_a_log(key, part):
    lowest = jnp.log(jnp.float32(2.0) / LEN)
    spread = jax.random.uniform(key, (NS, DI), jnp.float32)
    return (lowest + spread * (jnp.log(jnp.float32(2.0)) - lowest)).astype(jnp.bfloat16)


def set_ends(array, stream_key, low, top_value):
    longest = array.shape.index(max(array.shape))
    spots = []
    for shift in (0, 1):
        where = [jax.random.randint(jax.random.fold_in(stream_key, axis), (), 0, length) for axis, length in enumerate(array.shape)]
        where[longest] = (where[longest] + shift) % array.shape[longest]
        spots.append(tuple(where))
    return array.at[spots[0]].set(low).at[spots[1]].set(top_value)


def levels(stream_key, shape, shards, low, high):
    factor_of, own = 1.0, jax.random.fold_in(stream_key, 6)
    for dim, blocks in shards:
        heights = jnp.exp(jax.random.uniform(jax.random.fold_in(own, dim), (blocks,), jnp.float32, low / len(shards), high / len(shards)))
        factor_of = factor_of * jnp.repeat(heights, shape[dim] // blocks).reshape([-1 if axis == dim else 1 for axis in range(len(shape))])
    return factor_of


def centred(key, shape, width, limit, cuts=(), kind=jnp.bfloat16):
    level = levels(key, shape, cuts, -0.22, 0.18) if cuts else 1.0
    drawn = jax.random.normal(key, shape, jnp.float32) * width * level
    return jnp.minimum(jnp.maximum(drawn, -limit), limit).astype(kind)


def setup_inputs(seed: int = 0) -> dict:
    arg_keys = jax.random.split(jax.random.key(seed), 24)
    block_input = centred(arg_keys[0], (ROWS, D), 1.0, 6.0, ((0, 16),), jnp.float32)
    cotangent = centred(arg_keys[1], (ROWS, D), 1.0, 6.0, ((0, 16),), jnp.float32)
    lengths = draw_lengths(jax.random.fold_in(arg_keys[23], 71), 0)
    offsets = set_ends(jax.random.randint(arg_keys[3], (N_SEQS,), W, 2 * W), jax.random.fold_in(arg_keys[3], 1), W, (2 * W) - 1).astype(jnp.int32)
    ssm_state = centred(arg_keys[4], (N_SEQS, NS, DI), 1.0, 6.0, ((0, 4), (2, 8)))
    conv_state = centred(arg_keys[5], (N_SEQS, KC - 1, DI), 1.0, 6.0, ((0, 4), (2, 8)))
    kv_cache = centred(arg_keys[6], (N_SEQS, 2, W, D), 1.0, 6.0, ((0, 4), (2, 4), (3, 2)))
    norm_gains = jnp.clip(1.0 + 0.1 * jax.random.normal(arg_keys[7], (4, D), jnp.float32), 0.5, 1.5).astype(jnp.bfloat16)
    w_in = centred(arg_keys[8], (2, D, DI), D ** -0.5, 0.15625, ((2, 8),))
    conv_weight = centred(arg_keys[9], (KC, DI), KC ** -0.5, 3.0, ((1, 8),))
    conv_bias = centred(arg_keys[10], (DI,), 0.5, 3.0, ((0, 8),))
    x_proj = centred(arg_keys[11], (P_SIZE, DI), DI ** -0.5, 0.109375, ((1, 8),))
    dt_proj = centred(arg_keys[12], (R, DI), R ** -0.5, 0.625, ((1, 8),))
    dt_bias = jnp.clip(-5.0 + 2.0 * jax.random.uniform(arg_keys[13], (DI,), jnp.float32) ** levels(arg_keys[13], (DI,), ((0, 8),), -0.2, 0.2), -5.0, -3.0).astype(jnp.bfloat16)
    a_log = draw_a_log(jax.random.fold_in(arg_keys[23], 71), 0)
    d_skip = jnp.clip(0.5 + 1.0 * jax.random.uniform(arg_keys[15], (DI,), jnp.float32) ** levels(arg_keys[15], (DI,), ((0, 8),), -0.2, 0.2), 0.5, 1.5).astype(jnp.bfloat16)
    mamba_out = centred(arg_keys[16], (DI, D), DI ** -0.5, 0.109375, ((0, 8),))
    ffn1_gate_up = centred(arg_keys[17], (2, D, FF), D ** -0.5, 0.15625, ((2, 8),))
    ffn1_down = centred(arg_keys[18], (FF, D), FF ** -0.5, 0.09375, ((0, 8),))
    qkv_proj = centred(arg_keys[19], (3, D, D), D ** -0.5, 0.15625, ((1, 4), (2, 2)))
    attn_out = centred(arg_keys[20], (D, D), (max(D * 4 // W, 1)) ** -0.5, 3.5, ((0, 2), (1, 4)))
    ffn2_gate_up = centred(arg_keys[21], (2, D, FF), D ** -0.5, 0.15625, ((2, 8),))
    ffn2_down = centred(arg_keys[22], (FF, D), FF ** -0.5, 0.09375, ((0, 8),))
    return dict(block_input=block_input, cotangent=cotangent, lengths=lengths, offsets=offsets, ssm_state=ssm_state, conv_state=conv_state, kv_cache=kv_cache, norm_gains=norm_gains, w_in=w_in, conv_weight=conv_weight, conv_bias=conv_bias, x_proj=x_proj, dt_proj=dt_proj, dt_bias=dt_bias, a_log=a_log, d_skip=d_skip, mamba_out=mamba_out, ffn1_gate_up=ffn1_gate_up, ffn1_down=ffn1_down, qkv_proj=qkv_proj, attn_out=attn_out, ffn2_gate_up=ffn2_gate_up, ffn2_down=ffn2_down)


@jax.custom_vjp
def low(v):
    return lax.optimization_barrier(v.astype(jnp.bfloat16)).astype(jnp.float32)

@jax.custom_vjp
def low_back(v):
    return v

def low_keep(v):
    return (low(v), None)

def low_pass(kept, grad):
    return (grad,)

def back_keep(v):
    return (v, None)

def back_low(kept, grad):
    return (low(grad),)
low.defvjp(low_keep, low_pass)
low_back.defvjp(back_keep, back_low)
HIGHEST = lax.Precision.HIGHEST
EPSILON = 1e-05
ROPE_BASE = 10000.0
NEG_BIG = -1e+30

def matmul(left_op, right_op):
    return jnp.dot(left_op, right_op, precision=HIGHEST, preferred_element_type=jnp.float32)

def rms_norm(values, norm_gain):
    return values * lax.rsqrt(lax.optimization_barrier(jnp.mean(values * values, axis=-1, keepdims=True)) + EPSILON) * norm_gain

def rotate(values, positions):
    count_rows = values.shape[0]
    by_head = values.reshape(count_rows, -1, HD)
    half_dim = HD // 2
    frequency = ROPE_BASE ** (-(jnp.arange(half_dim, dtype=jnp.float32) * 2.0 / HD))
    angles = positions.astype(jnp.float32)[:, None] * frequency[None, :]
    cosine = jnp.cos(angles)[:, None, :]
    sine_part = jnp.sin(angles)[:, None, :]
    first_half = by_head[..., :half_dim]
    second_half = by_head[..., half_dim:]
    turned = jnp.concatenate([first_half * cosine - second_half * sine_part, second_half * cosine + first_half * sine_part], axis=-1)
    return turned.reshape(count_rows, -1)

def scan_tokens(entering, step_size, in_coef, out_coef, conv_out, decay_rate):

    def advance(ssm_now, token_row):
        step_row, in_row, out_row, input_row = token_row
        ssm_now = jnp.exp(step_row[None, :] * decay_rate) * ssm_now + in_row[:, None] * (step_row * input_row)[None, :]
        return (ssm_now, lax.optimization_barrier(jnp.sum(out_row[:, None] * ssm_now, axis=0)))
    return lax.scan(advance, entering, (step_size, in_coef, out_coef, conv_out))

def blocked_scan(entering, step_size, in_coef, out_coef, conv_out, decay_rate):
    block_count = step_size.shape[0] // TOK_DEV

    def split_rows(array_in):
        return array_in.reshape(block_count, TOK_DEV, array_in.shape[-1])
    one_block = jax.checkpoint(scan_tokens)

    def per_block(ssm_now, block_rows):
        return one_block(ssm_now, block_rows[0], block_rows[1], block_rows[2], block_rows[3], decay_rate)
    final_state, outputs = lax.scan(per_block, entering, (split_rows(step_size), split_rows(in_coef), split_rows(out_coef), split_rows(conv_out)))
    return (final_state, outputs.reshape(-1, conv_out.shape[-1]))

def feed_forward(resid, norm_gain, gate_up, down_proj, is_valid):
    normed = low(rms_norm(resid, norm_gain))
    gate_lin = low_back(matmul(normed, gate_up[0]))
    up_lin = low_back(matmul(normed, gate_up[1]))
    hidden = low(jax.nn.silu(gate_lin) * up_lin)
    return resid + is_valid * low_back(matmul(hidden, down_proj))

def attend(first_row, queries, all_keys, all_values, length):
    query_block = queries.shape[0] if queries.shape[0] < 512 else 512
    q_rows = lax.dynamic_slice_in_dim(queries, first_row, query_block, 0).reshape(query_block, H, HD)
    k_rows = lax.dynamic_slice_in_dim(all_keys, first_row, W + query_block, 0).reshape(W + query_block, H, HD)
    v_rows = lax.dynamic_slice_in_dim(all_values, first_row, W + query_block, 0).reshape(W + query_block, H, HD)
    scores = low_back(jnp.einsum('qhd,khd->hqk', q_rows, k_rows, precision=HIGHEST) * HD ** (-0.5))
    query_pos = first_row + jnp.arange(query_block, dtype=jnp.int32)[:, None]
    key_pos = first_row - W + jnp.arange(W + query_block, dtype=jnp.int32)[None, :]
    in_window = (key_pos > query_pos - W) & (key_pos <= query_pos) & (key_pos < length)
    scores = jnp.where(in_window[None], scores, NEG_BIG)
    attn_prob = jax.nn.softmax(scores, axis=-1)
    attended = jnp.einsum('hqk,khd->qhd', low(attn_prob), v_rows, precision=HIGHEST)
    return low(low_back(attended)).reshape(query_block, H * HD)

def attention(resid, norm_gain, qkv_proj, attn_out, kv_past, length, offset, is_valid):
    seq_rows = resid.shape[0]
    positions = offset + jnp.arange(seq_rows, dtype=jnp.int32)
    normed = low(rms_norm(resid, norm_gain))
    queries = low(rotate(low_back(matmul(normed, qkv_proj[0])), positions))
    keys_new = low(rotate(low_back(matmul(normed, qkv_proj[1])), positions))
    values_new = low(low_back(matmul(normed, qkv_proj[2])))
    all_keys = jnp.concatenate([kv_past[0], keys_new], axis=0)
    all_values = jnp.concatenate([kv_past[1], values_new], axis=0)
    new_cache = jnp.stack([lax.dynamic_slice_in_dim(all_keys, length, W, 0), lax.dynamic_slice_in_dim(all_values, length, W, 0)])
    query_block = min(512, seq_rows)
    starts = jnp.arange(0, seq_rows, query_block, dtype=jnp.int32)
    checked = jax.checkpoint(attend)
    blocks_out = lax.map(lambda first_row: checked(first_row, queries, all_keys, all_values, length), starts)
    attended = blocks_out.reshape(seq_rows, H * HD)
    return (resid + is_valid * low_back(matmul(attended, attn_out)), new_cache)

def one_sequence(params, seq_input, length, offset, kv_past, ssm_start, conv_start):
    norm_gains, w_in, conv_weight, conv_bias, x_proj, dt_proj, dt_bias, a_log, d_skip, mamba_out, ffn1_gate_up, ffn1_down, qkv_proj, attn_out, ffn2_gate_up, ffn2_down = params
    seq_rows = seq_input.shape[0]
    row_index = jnp.arange(seq_rows, dtype=jnp.int32)
    is_valid = (row_index < length).astype(jnp.float32)[:, None]
    normed = low(rms_norm(seq_input, norm_gains[0]))
    x_lin = low_back(matmul(normed, w_in[0]))
    z_lin = low_back(matmul(normed, w_in[1]))
    x_low = low(x_lin)
    padded = jnp.concatenate([conv_start, x_low], axis=0)
    conv_pre = conv_bias + sum((conv_weight[tap_at] * padded[tap_at:tap_at + seq_rows] for tap_at in range(KC)))
    conv_out = jax.nn.silu(conv_pre)
    projected = low_back(matmul(low(conv_out), x_proj.T))
    dt_low = low(projected[:, :R])
    in_coef = projected[:, R:R + NS]
    out_coef = projected[:, R + NS:]
    dt_lin = low_back(matmul(dt_low, dt_proj) + dt_bias)
    step_size = jax.nn.softplus(dt_lin) * is_valid
    decay_rate = -jnp.exp(a_log)
    final_state, scanned = blocked_scan(ssm_start, step_size, in_coef, out_coef, conv_out, decay_rate)
    mixed_out = scanned + d_skip * conv_out
    gated_low = low(mixed_out * jax.nn.silu(z_lin))
    after_mamba = seq_input + is_valid * low_back(matmul(gated_low, mamba_out))
    new_conv = lax.dynamic_slice_in_dim(padded, length, KC - 1, 0)
    after_ffn_one = feed_forward(after_mamba, norm_gains[1], ffn1_gate_up, ffn1_down, is_valid)
    after_attn, new_cache = attention(after_ffn_one, norm_gains[2], qkv_proj, attn_out, kv_past, length, offset, is_valid)
    block_out = feed_forward(after_attn, norm_gains[3], ffn2_gate_up, ffn2_down, is_valid)
    return (block_out, (final_state, new_conv, new_cache))

def reference(block_input, cotangent, lengths, offsets, ssm_state, conv_state, kv_cache, norm_gains, w_in, conv_weight, conv_bias, x_proj, dt_proj, dt_bias, a_log, d_skip, mamba_out, ffn1_gate_up, ffn1_down, qkv_proj, attn_out, ffn2_gate_up, ffn2_down):
    params = tuple((weight.astype(jnp.float32) for weight in (norm_gains, w_in, conv_weight, conv_bias, x_proj, dt_proj, dt_bias, a_log, d_skip, mamba_out, ffn1_gate_up, ffn1_down, qkv_proj, attn_out, ffn2_gate_up, ffn2_down)))
    checked_seq = jax.checkpoint(one_sequence)

    def layer_fn(params, inputs_all, kv_all, ssm_all, conv_all):

        def seq_step(unused, seq_data):
            return (unused, checked_seq(params, *seq_data))
        _, (outputs, extras) = lax.scan(seq_step, jnp.zeros((), jnp.float32), (inputs_all.reshape(N_SEQS, LEN, D), lengths, offsets, kv_all, ssm_all, conv_all))
        return (outputs.reshape(ROWS, D), extras)
    block_output, pullback, extras = jax.vjp(layer_fn, params, block_input.astype(jnp.float32), kv_cache.astype(jnp.float32), ssm_state.astype(jnp.float32), conv_state.astype(jnp.float32), has_aux=True)
    grad_params, input_grad, cache_grad, ssm_grad, conv_grad = pullback(cotangent.astype(jnp.float32))
    new_ssm, new_conv, new_cache = extras
    return (block_output, input_grad, new_ssm.astype(jnp.bfloat16), new_conv.astype(jnp.bfloat16), new_cache.astype(jnp.bfloat16), ssm_grad, conv_grad, cache_grad, grad_params[0], grad_params[1], grad_params[2], grad_params[3], grad_params[4], grad_params[5], grad_params[6], grad_params[7], grad_params[8], grad_params[9], grad_params[10], grad_params[11], grad_params[12], grad_params[13], grad_params[14], grad_params[15])
```

```python
import jax
import jax.numpy as jnp
from jax import lax
from jax.experimental import pallas as pl
from jax.experimental.pallas import tpu as pltpu
from jax.sharding import PartitionSpec as P

HD = 128
EPSILON = 1e-05
ROPE_BASE = 10000.0
NEG_BIG = -1e30
DIRECT_MAX = 4
BF = jnp.bfloat16
F32 = jnp.float32


def matmul(left_op, right_op):
    return jnp.dot(left_op, right_op, preferred_element_type=F32)


def matmul_tn(left_op, right_op):
    return lax.dot_general(left_op, right_op, (((0,), (0,)), ((), ())), preferred_element_type=F32)


def matmul_nt(left_op, right_op):
    return lax.dot_general(left_op, right_op, (((1,), (1,)), ((), ())), preferred_element_type=F32)


def direct():
    return lax.axis_size("blk") <= DIRECT_MAX


def from_ahead(value, steps):
    count = lax.axis_size("blk")
    return lax.ppermute(value, "blk", [((i + steps) % count, i) for i in range(count)])


def to_ahead(value, steps):
    count = lax.axis_size("blk")
    return lax.ppermute(value, "blk", [(i, (i + steps) % count) for i in range(count)])


def mp_swap(value):
    return lax.ppermute(value, "mp", [(0, 1), (1, 0)])


def by_order(first, own, other):
    return jnp.stack([jnp.where(first, own, other), jnp.where(first, other, own)])


def blk_ordered(pieces):
    count = len(pieces)
    dev_index = lax.axis_index("blk")
    ordered = []
    for place in range(count):
        distance = (place - dev_index) % count
        chosen = pieces[0]
        for steps in range(1, count):
            chosen = jnp.where(distance == steps, pieces[steps], chosen)
        ordered.append(chosen)
    return ordered


def gather_rows(rows, ordered):
    if not direct():
        return lax.all_gather(rows, ("blk", "mp"), axis=0, tiled=True)
    count = lax.axis_size("blk")
    pieces = [rows] + [from_ahead(rows, steps) for steps in range(1, count)]
    others = [mp_swap(piece) for piece in pieces]
    if not ordered:
        return jnp.concatenate(pieces + others, axis=0)
    first = lax.axis_index("mp") == 0
    own_in, other_in = (blk_ordered(pieces), blk_ordered(others))
    laid = []
    for own, other in zip(own_in, other_in):
        laid += [jnp.where(first, own, other), jnp.where(first, other, own)]
    return jnp.concatenate(laid, axis=0)


def scatter_rows(partial, ordered):
    if not direct():
        return lax.psum_scatter(
            partial.astype(BF), ("blk", "mp"), scatter_dimension=0, tiled=True
        ).astype(F32)
    count = lax.axis_size("blk")
    rows = partial.shape[0] // (2 * count)
    width = partial.shape[1]
    dev_index = lax.axis_index("blk")
    part = lax.axis_index("mp")
    if ordered:
        split = partial.astype(BF).reshape(count, 2, rows, width)
        mine = lax.dynamic_index_in_dim(split, part, 1, keepdims=False)
        theirs = lax.dynamic_index_in_dim(split, 1 - part, 1, keepdims=False)
    else:
        split = partial.astype(BF).reshape(2, count, rows, width)
        mine, theirs = (split[0], split[1])
    both = (mine.astype(F32) + mp_swap(theirs).astype(F32)).astype(BF)
    total = None
    for steps in range(count - 1, -1, -1):
        if ordered:
            chunk = lax.dynamic_index_in_dim(both, (dev_index + steps) % count, 0, keepdims=False)
        else:
            chunk = both[steps]
        arrived = (to_ahead(chunk, steps) if steps else chunk).astype(F32)
        total = arrived if total is None else total + arrived
    return total


def sum_small(partial):
    if not direct():
        return lax.psum(partial.astype(BF), ("blk", "mp")).astype(F32)
    count = lax.axis_size("blk")
    part = lax.axis_index("mp")
    split = partial.reshape(2, partial.shape[0] // 2, partial.shape[1])
    mine = lax.dynamic_index_in_dim(split, part, 0, keepdims=False)
    theirs = lax.dynamic_index_in_dim(split, 1 - part, 0, keepdims=False)
    both = (mine + mp_swap(theirs)).astype(BF)
    total = both.astype(F32)
    for steps in range(1, count):
        total = total + from_ahead(both, steps).astype(F32)
    return by_order(part == 0, total, mp_swap(total)).reshape(partial.shape)


def blk_all(value):
    if not direct():
        return lax.all_gather(value, "blk", axis=0)
    return jnp.stack([value] + [from_ahead(value, s) for s in range(1, lax.axis_size("blk"))])


def blk_gather_cols(value):
    if not direct():
        return lax.all_gather(value, "blk", axis=1, tiled=True)
    pieces = [value] + [from_ahead(value, s) for s in range(1, lax.axis_size("blk"))]
    return jnp.concatenate(blk_ordered(pieces), axis=1)


def blk_gather_rows(value):
    if not direct():
        return lax.all_gather(value, "blk", axis=0, tiled=True)
    pieces = [value] + [from_ahead(value, s) for s in range(1, lax.axis_size("blk"))]
    return jnp.concatenate(blk_ordered(pieces), axis=0)


def blk_scatter(partial, axis):
    count = lax.axis_size("blk")
    if not direct():
        return lax.psum_scatter(partial, "blk", scatter_dimension=axis, tiled=True).astype(F32)
    size = partial.shape[axis] // count
    dev_index = lax.axis_index("blk")
    total = None
    for steps in range(count - 1, -1, -1):
        chunk = lax.dynamic_slice_in_dim(partial, ((dev_index + steps) % count) * size, size, axis)
        arrived = (to_ahead(chunk, steps) if steps else chunk).astype(F32)
        total = arrived if total is None else total + arrived
    return total


def seq_sum(value):
    low = value.astype(BF)
    rows = low.shape[0]
    if lax.axis_size("seqs") != 4 or rows % 8:
        return lax.psum(low, "seqs").astype(F32)
    index = lax.axis_index("seqs")
    bits = (index % 2, index // 2)
    pairs = ([(0, 1), (1, 0), (2, 3), (3, 2)], [(0, 2), (2, 0), (1, 3), (3, 1)])

    def exchange(array, way):
        return lax.ppermute(array, "seqs", pairs[way])

    def halve(array, way):
        split = array.reshape(2, array.shape[0] // 2, array.shape[1])
        keep = lax.dynamic_index_in_dim(split, bits[way], 0, keepdims=False)
        send = lax.dynamic_index_in_dim(split, 1 - bits[way], 0, keepdims=False)
        return (keep.astype(F32) + exchange(send, way).astype(F32)).astype(BF)

    def double(array, way):
        pair = by_order(bits[way] == 0, array, exchange(array, way))
        return pair.reshape(2 * array.shape[0], array.shape[1])

    halves = []
    for begin, first, second in ((0, 0, 1), (rows // 2, 1, 0)):
        piece = low[begin : begin + rows // 2]
        piece = halve(halve(piece, first), second)
        halves.append(double(double(piece, second), first))
    return jnp.concatenate(halves, axis=0).astype(F32)


def norm_forward(values, norm_gain):
    inverse = lax.rsqrt(jnp.mean(values * values, axis=-1, keepdims=True) + EPSILON)
    unit_rows = values * inverse
    return ((unit_rows * norm_gain).astype(BF), unit_rows, inverse)


def norm_backward(grad_out, unit_rows, inverse, norm_gain):
    grad_unit = grad_out * norm_gain
    grad_gain = jnp.sum(grad_out * unit_rows, axis=0)
    grad_in = inverse * (
        grad_unit - unit_rows * jnp.mean(grad_unit * unit_rows, axis=-1, keepdims=True)
    )
    return (grad_in, grad_gain)


def silu_slope(values):
    logistic = jax.nn.sigmoid(values)
    return logistic * (1.0 + values * (1.0 - logistic))


def rotation_tables(positions):
    half_dim = HD // 2
    frequency = ROPE_BASE ** (-(jnp.arange(half_dim, dtype=F32) * 2.0 / HD))
    angles = positions.astype(F32)[:, None] * frequency[None, :]
    return (jnp.cos(angles), jnp.sin(angles))


def rotate(values, cosine, sine_part, direction):
    count_rows = values.shape[0]
    by_head = values.reshape(count_rows, -1, HD)
    half_dim = HD // 2
    cos_rows = cosine[:, None, :]
    sin_rows = direction * sine_part[:, None, :]
    first_half = by_head[..., :half_dim]
    second_half = by_head[..., half_dim:]
    turned = jnp.concatenate(
        [
            first_half * cos_rows - second_half * sin_rows,
            second_half * cos_rows + first_half * sin_rows,
        ],
        axis=-1,
    )
    return turned.reshape(count_rows, -1)


def wide(array, times):
    return array if times == 1 else jnp.concatenate([array] * times, axis=1)


def scan_fwd_kernel(
    step_ref, u_ref, in_ref, out_ref, dec_ref, h0_ref, y_ref, hp_ref, hf_ref, h_scr
):
    @pl.when(pl.program_id(0) == 0)
    def _():
        h_scr[...] = h0_ref[...]

    decay = dec_ref[...]
    times = decay.shape[1] // in_ref.shape[2]

    def group(turn, state):
        base = pl.multiple_of(turn * 8, 8)
        steps = step_ref[pl.ds(base, 8), :]
        drives = u_ref[pl.ds(base, 8), :]
        outs = []
        for j in range(8):
            hp_ref[base + j] = state
            shrink = jnp.exp(steps[j : j + 1, :] * decay)
            state = shrink * state + wide(in_ref[base + j], times) * drives[j : j + 1, :]
            outs.append(jnp.sum(wide(out_ref[base + j], times) * state, axis=0, keepdims=True))
        y_ref[pl.ds(base, 8), :] = jnp.concatenate(outs, axis=0)
        return state

    state = lax.fori_loop(0, step_ref.shape[0] // 8, group, h_scr[...])
    h_scr[...] = state
    hf_ref[...] = state


def scan_bwd_kernel(
    step_ref,
    u_ref,
    gy_ref,
    in_ref,
    out_ref,
    hp_ref,
    dec_ref,
    gu_ref,
    gs_ref,
    gin_ref,
    gout_ref,
    gdec_ref,
    gh_ref,
    a_scr,
    d_scr,
):
    @pl.when(pl.program_id(0) == 0)
    def _():
        a_scr[...] = jnp.zeros_like(a_scr)
        d_scr[...] = jnp.zeros_like(d_scr)

    decay = dec_ref[...]
    lanes = in_ref.shape[2]
    times = decay.shape[1] // lanes
    groups = step_ref.shape[0] // 8

    def fold(array):
        total = array[:, :lanes]
        for k in range(1, times):
            total = total + array[:, k * lanes : (k + 1) * lanes]
        return total

    def group(turn, carried):
        adj, grad_decay = carried
        base = pl.multiple_of((groups - 1 - turn) * 8, 8)
        steps = step_ref[pl.ds(base, 8), :]
        drives = u_ref[pl.ds(base, 8), :]
        grads = gy_ref[pl.ds(base, 8), :]
        gus, gss = ([], [])
        for j in range(7, -1, -1):
            step_row, u_row, gy_row = (
                steps[j : j + 1, :],
                drives[j : j + 1, :],
                grads[j : j + 1, :],
            )
            in_now = wide(in_ref[base + j], times)
            before = hp_ref[base + j]
            shrink = jnp.exp(step_row * decay)
            kept = shrink * before
            state = kept + in_now * u_row
            adj = adj + wide(out_ref[base + j], times) * gy_row
            gout_ref[base + j] = fold(state * gy_row)
            gin_ref[base + j] = fold(adj * u_row)
            gus.append(jnp.sum(adj * in_now, axis=0, keepdims=True))
            grad_exp = adj * kept
            gss.append(jnp.sum(grad_exp * decay, axis=0, keepdims=True))
            grad_decay = grad_decay + grad_exp * step_row
            adj = shrink * adj
        gu_ref[pl.ds(base, 8), :] = jnp.concatenate(gus[::-1], axis=0)
        gs_ref[pl.ds(base, 8), :] = jnp.concatenate(gss[::-1], axis=0)
        return (adj, grad_decay)

    adj, grad_decay = lax.fori_loop(0, groups, group, (a_scr[...], d_scr[...]))
    a_scr[...] = adj
    d_scr[...] = grad_decay
    gh_ref[...] = adj
    gdec_ref[...] = grad_decay


def scan_forward(entering, step, drive, in_b, out_b, decay):
    rows, chans = step.shape
    states, lanes = (decay.shape[0], in_b.shape[2])
    block = min(128, rows)
    row_spec = pl.BlockSpec((block, chans), lambda i: (i, 0))
    coef_spec = pl.BlockSpec((block, states, lanes), lambda i: (i, 0, 0))
    hist_spec = pl.BlockSpec((block, states, chans), lambda i: (i, 0, 0))
    fixed = pl.BlockSpec((states, chans), lambda i: (0, 0))
    return pl.pallas_call(
        scan_fwd_kernel,
        grid=(rows // block,),
        in_specs=[row_spec, row_spec, coef_spec, coef_spec, fixed, fixed],
        out_specs=[row_spec, hist_spec, fixed],
        out_shape=[
            jax.ShapeDtypeStruct((rows, chans), F32),
            jax.ShapeDtypeStruct((rows, states, chans), F32),
            jax.ShapeDtypeStruct((states, chans), F32),
        ],
        scratch_shapes=[pltpu.VMEM((states, chans), F32)],
        name="scan_fwd",
    )(step, drive, in_b, out_b, decay, entering)


def scan_backward(step, drive, grad_y, in_b, out_b, before, decay):
    rows, chans = step.shape
    states, lanes = (decay.shape[0], in_b.shape[2])
    block = min(128, rows)
    last = rows // block - 1
    row_spec = pl.BlockSpec((block, chans), lambda i: (last - i, 0))
    coef_spec = pl.BlockSpec((block, states, lanes), lambda i: (last - i, 0, 0))
    hist_spec = pl.BlockSpec((block, states, chans), lambda i: (last - i, 0, 0))
    fixed = pl.BlockSpec((states, chans), lambda i: (0, 0))
    return pl.pallas_call(
        scan_bwd_kernel,
        grid=(rows // block,),
        in_specs=[row_spec, row_spec, row_spec, coef_spec, coef_spec, hist_spec, fixed],
        out_specs=[row_spec, row_spec, coef_spec, coef_spec, fixed, fixed],
        out_shape=[
            jax.ShapeDtypeStruct((rows, chans), F32),
            jax.ShapeDtypeStruct((rows, chans), F32),
            jax.ShapeDtypeStruct((rows, states, lanes), F32),
            jax.ShapeDtypeStruct((rows, states, lanes), F32),
            jax.ShapeDtypeStruct((states, chans), F32),
            jax.ShapeDtypeStruct((states, chans), F32),
        ],
        scratch_shapes=[pltpu.VMEM((states, chans), F32), pltpu.VMEM((states, chans), F32)],
        name="scan_bwd",
    )(step, drive, grad_y, in_b, out_b, before, decay)


def masked_scores(queries, keys, allowed):
    scores = lax.dot_general(
        queries, keys, (((1,), (1,)), ((), ())), preferred_element_type=F32
    ) * HD ** (-0.5)
    return jnp.where(allowed, scores, NEG_BIG)


def allowed_keys(qpos_ref, kpos_ref, window):
    query_at, key_at = (qpos_ref[...], kpos_ref[...])
    return (key_at > query_at - window) & (key_at <= query_at)


def attend_fwd_kernel(window, q_ref, k_ref, v_ref, qpos_ref, kpos_ref, o_ref, stat_ref):
    allowed = allowed_keys(qpos_ref, kpos_ref, window)
    lane = lax.broadcasted_iota(jnp.int32, stat_ref.shape, 1)
    stats = jnp.zeros(stat_ref.shape, F32)
    for head in range(q_ref.shape[1] // HD):
        cols = slice(head * HD, (head + 1) * HD)
        scores = masked_scores(q_ref[:, cols], k_ref[:, cols], allowed)
        row_max = jnp.max(scores, axis=1, keepdims=True)
        weights = jnp.exp(scores - row_max)
        row_sum = jnp.sum(weights, axis=1, keepdims=True)
        o_ref[:, cols] = jnp.dot(weights.astype(BF), v_ref[:, cols], preferred_element_type=F32)
        stats = jnp.where(lane == head, row_max, stats)
        stats = jnp.where(lane == head + HD // 2, row_sum, stats)
    stat_ref[...] = stats


def attend_bwd_kernel(
    window, q_ref, k_ref, v_ref, go_ref, stat_ref, qpos_ref, kpos_ref, gq_ref, gk_ref, gv_ref
):
    @pl.when(pl.program_id(0) == 0)
    def _():
        gk_ref[...] = jnp.zeros_like(gk_ref)
        gv_ref[...] = jnp.zeros_like(gv_ref)

    allowed = allowed_keys(qpos_ref, kpos_ref, window)
    scale = HD ** (-0.5)
    for head in range(q_ref.shape[1] // HD):
        cols = slice(head * HD, (head + 1) * HD)
        queries, keys, grads = (q_ref[:, cols], k_ref[:, cols], go_ref[:, cols])
        scores = masked_scores(queries, keys, allowed)
        probs = jnp.exp(scores - stat_ref[:, head : head + 1])
        grad_prob = lax.dot_general(
            grads, v_ref[:, cols], (((1,), (1,)), ((), ())), preferred_element_type=F32
        )
        delta = stat_ref[:, head + HD // 2 : head + HD // 2 + 1]
        grad_scores = (probs * (grad_prob - delta)).astype(BF)
        gq_ref[:, cols] = jnp.dot(grad_scores, keys, preferred_element_type=F32) * scale
        gk_ref[:, cols] += matmul_tn(grad_scores, queries) * scale
        gv_ref[:, cols] += matmul_tn(probs.astype(BF), grads)


def attend_forward(queries, keys, values, query_pos, key_pos, window):
    rows, width = queries.shape
    count = keys.shape[0]
    block = min(256, rows)
    row_spec = pl.BlockSpec((block, width), lambda i: (i, 0))
    key_spec = pl.BlockSpec((count, width), lambda i: (0, 0))
    return pl.pallas_call(
        lambda *refs: attend_fwd_kernel(window, *refs),
        grid=(rows // block,),
        in_specs=[
            row_spec,
            key_spec,
            key_spec,
            pl.BlockSpec((block, 1), lambda i: (i, 0)),
            pl.BlockSpec((1, count), lambda i: (0, 0)),
        ],
        out_specs=[row_spec, pl.BlockSpec((block, HD), lambda i: (i, 0))],
        out_shape=[
            jax.ShapeDtypeStruct((rows, width), F32),
            jax.ShapeDtypeStruct((rows, HD), F32),
        ],
        name="attend_fwd",
    )(queries, keys, values, query_pos, key_pos)


def attend_backward(queries, keys, values, grads, stats, query_pos, key_pos, window):
    rows, width = queries.shape
    count = keys.shape[0]
    block = min(256, rows)
    row_spec = pl.BlockSpec((block, width), lambda i: (i, 0))
    key_spec = pl.BlockSpec((count, width), lambda i: (0, 0))
    return pl.pallas_call(
        lambda *refs: attend_bwd_kernel(window, *refs),
        grid=(rows // block,),
        in_specs=[
            row_spec,
            key_spec,
            key_spec,
            row_spec,
            pl.BlockSpec((block, HD), lambda i: (i, 0)),
            pl.BlockSpec((block, 1), lambda i: (i, 0)),
            pl.BlockSpec((1, count), lambda i: (0, 0)),
        ],
        out_specs=[row_spec, key_spec, key_spec],
        out_shape=[
            jax.ShapeDtypeStruct((rows, width), F32),
            jax.ShapeDtypeStruct((count, width), F32),
            jax.ShapeDtypeStruct((count, width), F32),
        ],
        name="attend_bwd",
    )(queries, keys, values, grads, stats, query_pos, key_pos)


def ffn_forward(rows, gain, gate_up, down, valid):
    normed, unit, inverse = norm_forward(rows, gain)
    full = gather_rows(normed, False)
    gate, up = (matmul(full, gate_up[0]), matmul(full, gate_up[1]))
    hidden = (jax.nn.silu(gate) * up).astype(BF)
    after = rows + valid * scatter_rows(matmul(hidden, down), False)
    return (after, (full, unit, inverse, gate, up, hidden))


def ffn_backward(grad_after, kept, gain, gate_up, down, valid):
    full, unit, inverse, gate, up, hidden = kept
    branch = gather_rows((valid * grad_after).astype(BF), False)
    grad_hidden = matmul_nt(branch, down)
    grad_gate = (grad_hidden * up * silu_slope(gate)).astype(BF)
    grad_up = (grad_hidden * jax.nn.silu(gate)).astype(BF)
    grad_normed = scatter_rows(
        matmul_nt(grad_gate, gate_up[0]) + matmul_nt(grad_up, gate_up[1]), False
    )
    grad_in, grad_gain = norm_backward(grad_normed, unit, inverse, gain)
    grad_down = matmul_tn(hidden, branch)
    grad_gate_up = jnp.concatenate([matmul_tn(full, grad_gate), matmul_tn(full, grad_up)], axis=0)
    return (grad_after + grad_in, grad_gain, grad_gate_up, grad_down)


def shards(
    block_input,
    cotangent,
    lengths,
    offsets,
    ssm_state,
    conv_state,
    kv_cache,
    norm_gains,
    w_in,
    conv_weight,
    conv_bias,
    x_proj,
    dt_proj,
    dt_bias,
    a_log,
    d_skip,
    mamba_out,
    ffn1_gate_up,
    ffn1_down,
    qkv_proj,
    attn_out,
    ffn2_gate_up,
    ffn2_down,
):
    blocks = lax.axis_size("blk")
    dev_index = lax.axis_index("blk")
    part = lax.axis_index("mp")
    first = part == 0
    tok_rows, model = block_input.shape
    own_rows = tok_rows // 2
    total_rows = tok_rows * blocks
    seq_len = lengths[0]
    offset = offsets[0]
    window = kv_cache.shape[2] * blocks
    cache_rows = kv_cache.shape[2]

    qkv_full = lax.all_gather(qkv_proj, "blk", axis=1, tiled=True)
    out_full = lax.all_gather(attn_out, "blk", axis=1, tiled=True)

    gains = blk_gather_cols(norm_gains).astype(F32)
    rows_in = lax.dynamic_slice_in_dim(block_input, part * own_rows, own_rows, 0)
    grad_rows = lax.dynamic_slice_in_dim(cotangent, part * own_rows, own_rows, 0)
    own_pos = dev_index * tok_rows + part * own_rows + jnp.arange(own_rows, dtype=jnp.int32)
    valid = (own_pos < seq_len).astype(F32)[:, None]
    token_at = jnp.arange(total_rows, dtype=jnp.int32)
    valid_all = (token_at < seq_len).astype(F32)[:, None]

    normed_m, unit_m, inverse_m = norm_forward(rows_in, gains[0])
    full_m = gather_rows(normed_m, True)
    x_low = matmul(full_m, w_in[0]).astype(BF)
    z_lin = matmul(full_m, w_in[1])
    taps = conv_weight.shape[0]
    conv_w = conv_weight.astype(F32)
    padded = jnp.concatenate([conv_state[0], x_low], axis=0)
    padded_f = padded.astype(F32)
    conv_pre = conv_bias.astype(F32) + sum(
        (conv_w[k] * padded_f[k : k + total_rows] for k in range(taps))
    )
    conv_out = jax.nn.silu(conv_pre)
    conv_low = conv_out.astype(BF)
    rank = dt_proj.shape[0]
    states, chans = a_log.shape
    projected = sum_small(matmul_nt(conv_low, x_proj))
    dt_low = projected[:, :rank].astype(BF)
    lanes = min(chans, 128)
    spread = (total_rows, states, lanes)
    in_b = jnp.broadcast_to(projected[:, rank : rank + states, None], spread)
    out_b = jnp.broadcast_to(projected[:, rank + states :, None], spread)
    dt_lin = matmul(dt_low, dt_proj) + dt_bias.astype(F32)
    step = jax.nn.softplus(dt_lin) * valid_all
    decay = -jnp.exp(a_log.astype(F32))
    drive = step * conv_out
    scanned, before, final_state = scan_forward(
        ssm_state[0].astype(F32), step, drive, in_b, out_b, decay
    )
    skip = d_skip.astype(F32)
    mixed = scanned + skip * conv_out
    gated = (mixed * jax.nn.silu(z_lin)).astype(BF)
    rows_m = rows_in + valid * scatter_rows(matmul(gated, mamba_out), True)
    new_conv = lax.dynamic_slice_in_dim(padded, seq_len, taps - 1, 0)

    rows_one, kept_one = ffn_forward(rows_m, gains[1], ffn1_gate_up, ffn1_down, valid)

    normed_a, unit_a, inverse_a = norm_forward(rows_one, gains[2])
    full_a = gather_rows(normed_a, True)
    cosine, sine = rotation_tables(offset + token_at)
    q_low = rotate(matmul(full_a, qkv_full[0]), cosine, sine, 1.0).astype(BF)
    k_low = rotate(matmul(full_a, qkv_full[1]), cosine, sine, 1.0).astype(BF)
    v_low = matmul(full_a, qkv_full[2]).astype(BF)
    width = q_low.shape[1]
    heads = width // HD
    first_pos = dev_index * tok_rows

    def own_block(array):
        return lax.dynamic_slice_in_dim(array, first_pos, tok_rows, 0)

    keys = jnp.concatenate([kv_cache[0, 0], own_block(k_low)], axis=0)
    values = jnp.concatenate([kv_cache[0, 1], own_block(v_low)], axis=0)
    cache_at = dev_index * cache_rows - window + jnp.arange(cache_rows, dtype=jnp.int32)
    fresh_at = first_pos + jnp.arange(tok_rows, dtype=jnp.int32)
    fresh_at = jnp.where(fresh_at < seq_len, fresh_at, 2 * total_rows + window)
    key_pos = jnp.concatenate([cache_at, fresh_at])[None, :]
    query_pos = token_at[:, None]
    weighted, stats = attend_forward(q_low, keys, values, query_pos, key_pos, window)
    row_max = stats[:, :heads].T
    row_sum = stats[:, HD // 2 : HD // 2 + heads].T
    all_lse = blk_all(row_max + jnp.log(row_sum))
    top = jnp.max(all_lse, axis=0)
    lse = top + jnp.log(jnp.sum(jnp.exp(all_lse - top[None]), axis=0))
    share = jnp.exp(row_max - lse).T
    att_part = weighted.reshape(total_rows, heads, HD) * share[:, :, None]
    att_low = att_part.reshape(total_rows, width).astype(BF)
    rows_two = rows_one + valid * scatter_rows(matmul(att_low, out_full), True)

    rows_out, kept_two = ffn_forward(rows_two, gains[3], ffn2_gate_up, ffn2_down, valid)
    block_output = by_order(first, rows_out, mp_swap(rows_out)).reshape(tok_rows, model)

    grad_rows, gain_four, grad_gate_up_two, grad_down_two = ffn_backward(
        grad_rows, kept_two, gains[3], ffn2_gate_up, ffn2_down, valid
    )

    branch_a = gather_rows((valid * grad_rows).astype(BF), True)
    grad_att = matmul_nt(branch_a, out_full).astype(BF)
    delta_part = jnp.sum(
        (grad_att.astype(F32) * att_low.astype(F32)).reshape(total_rows, heads, HD), axis=-1
    )
    delta = jnp.sum(blk_all(delta_part.T), axis=0)
    gap = jnp.zeros((total_rows, HD // 2 - heads), F32)
    stats_b = jnp.concatenate([lse.T, gap, delta.T, gap], axis=1)
    grad_q, grad_keys, grad_values = attend_backward(
        q_low, keys, values, grad_att, stats_b, query_pos, key_pos, window
    )
    grad_q_low = rotate(grad_q, cosine, sine, -1.0).astype(BF)
    grad_k_low = rotate(
        grad_keys[cache_rows:], own_block(cosine), own_block(sine), -1.0
    ).astype(BF)
    grad_v_low = grad_values[cache_rows:].astype(BF)
    kv_cache_grad = jnp.stack([grad_keys[:cache_rows], grad_values[:cache_rows]])[None]
    grad_normed = matmul_nt(grad_q_low, qkv_full[0])
    grad_fresh = matmul_nt(grad_k_low, qkv_full[1]) + matmul_nt(grad_v_low, qkv_full[2])
    grad_normed = lax.dynamic_update_slice_in_dim(
        grad_normed, own_block(grad_normed) + grad_fresh, first_pos, 0
    )
    grad_in, gain_three = norm_backward(
        scatter_rows(grad_normed, True), unit_a, inverse_a, gains[2]
    )
    grad_rows = grad_rows + grad_in
    shard_cols = model // blocks

    def own_cols(array):
        return lax.dynamic_slice_in_dim(array, dev_index * shard_cols, shard_cols, 1)

    att_all = blk_gather_rows(blk_scatter(att_low, 0).astype(BF))
    grad_attn_out = matmul_tn(att_all, own_cols(branch_a))
    grad_q_own = blk_scatter(grad_q_low, 0).astype(BF)
    grad_qkv_all = blk_gather_rows(jnp.concatenate([grad_q_own, grad_k_low, grad_v_low], axis=1))
    normed_cols = own_cols(full_a)
    grad_qkv = jnp.concatenate(
        [matmul_tn(normed_cols, grad_qkv_all[:, k * width : (k + 1) * width]) for k in range(3)],
        axis=0,
    )

    grad_rows, gain_two, grad_gate_up_one, grad_down_one = ffn_backward(
        grad_rows, kept_one, gains[1], ffn1_gate_up, ffn1_down, valid
    )

    branch_m = gather_rows((valid * grad_rows).astype(BF), True)
    grad_mamba_out = matmul_tn(gated, branch_m)
    grad_gated = matmul_nt(branch_m, mamba_out)
    grad_mixed = grad_gated * jax.nn.silu(z_lin)
    grad_z = (grad_gated * mixed * silu_slope(z_lin)).astype(BF)
    grad_skip = jnp.sum(grad_mixed * conv_out, axis=0)
    grad_u, grad_step, grad_in_l, grad_out_l, grad_decay, grad_state = scan_backward(
        step, drive, grad_mixed, in_b, out_b, before, decay
    )
    grad_step = grad_step + grad_u * conv_out
    grad_dt = (grad_step * valid_all * jax.nn.sigmoid(dt_lin)).astype(BF)
    grad_dt_bias = jnp.sum(grad_dt.astype(F32), axis=0)
    grad_dt_proj = matmul_tn(dt_low, grad_dt)
    grad_proj = sum_small(
        jnp.concatenate(
            [matmul_nt(grad_dt, dt_proj), jnp.sum(grad_in_l, axis=-1), jnp.sum(grad_out_l, axis=-1)],
            axis=1,
        )
    ).astype(BF)
    grad_x_proj = matmul_tn(grad_proj, conv_low)
    grad_conv = grad_u * step + grad_mixed * skip + matmul(grad_proj, x_proj)
    grad_pre = grad_conv * silu_slope(conv_pre)
    grad_conv_b = jnp.sum(grad_pre, axis=0)
    grad_conv_w = jnp.stack(
        [jnp.sum(grad_pre * padded_f[k : k + total_rows], axis=0) for k in range(taps)]
    )
    grad_padded = sum(
        (
            jnp.pad(conv_w[k] * grad_pre, ((k, taps - 1 - k), (0, 0)))
            for k in range(taps)
        )
    )
    grad_x = grad_padded[taps - 1 :].astype(BF)
    grad_w_in = jnp.concatenate([matmul_tn(full_m, grad_x), matmul_tn(full_m, grad_z)], axis=0)
    grad_normed = scatter_rows(matmul_nt(grad_x, w_in[0]) + matmul_nt(grad_z, w_in[1]), True)
    grad_in, gain_one = norm_backward(grad_normed, unit_m, inverse_m, gains[0])
    grad_rows = grad_rows + grad_in
    input_grad = by_order(first, grad_rows, mp_swap(grad_rows)).reshape(tok_rows, model)

    fresh_kv = jnp.stack([k_low, v_low])
    if direct() and cache_rows >= total_rows:
        following = from_ahead(kv_cache[0, :, :total_rows], 1)
        following = jnp.where(dev_index == blocks - 1, fresh_kv, following)
        both = jnp.concatenate([kv_cache[0], following], axis=1)
        new_cache = lax.dynamic_slice_in_dim(both, seq_len, cache_rows, 1)
    else:
        cache_full = lax.all_gather(kv_cache[0], "blk", axis=1, tiled=True)
        both = jnp.concatenate([cache_full, fresh_kv], axis=1)
        new_cache = lax.dynamic_slice_in_dim(both, seq_len + dev_index * cache_rows, cache_rows, 1)

    gain_part = jnp.stack([gain_one, gain_two, gain_three, gain_four])
    gain_own = blk_scatter(gain_part, 1)
    gain_own = gain_own + mp_swap(gain_own)
    small = [
        (grad_x_proj, x_proj.shape),
        (grad_dt_proj, dt_proj.shape),
        (grad_decay * decay, a_log.shape),
        (grad_conv_w, conv_weight.shape),
        (gain_own, norm_gains.shape),
        (grad_conv_b[None], conv_bias.shape),
        (grad_dt_bias[None], dt_bias.shape),
        (grad_skip[None], d_skip.shape),
    ]
    packed = jnp.concatenate([piece for piece, _ in small], axis=0)
    packed = jnp.pad(packed, ((0, -packed.shape[0] % 64), (0, 0)))
    packed = seq_sum(packed)
    summed = []
    begin = 0
    for piece, shape in small:
        summed.append(packed[begin : begin + piece.shape[0]].reshape(shape))
        begin += piece.shape[0]
    sum_x_proj, sum_dt_proj, sum_a_log, sum_conv_w, sum_gains, sum_conv_b, sum_dt_bias, sum_skip = (
        summed
    )
    return (
        block_output,
        input_grad,
        final_state.astype(BF)[None],
        new_conv[None],
        new_cache[None],
        grad_state[None],
        grad_padded[: taps - 1][None],
        kv_cache_grad,
        sum_gains,
        seq_sum(grad_w_in).reshape(w_in.shape),
        sum_conv_w,
        sum_conv_b,
        sum_x_proj,
        sum_dt_proj,
        sum_dt_bias,
        sum_a_log,
        sum_skip,
        seq_sum(grad_mamba_out),
        seq_sum(grad_gate_up_one).reshape(ffn1_gate_up.shape),
        seq_sum(grad_down_one),
        seq_sum(grad_qkv).reshape(qkv_proj.shape),
        seq_sum(grad_attn_out),
        seq_sum(grad_gate_up_two).reshape(ffn2_gate_up.shape),
        seq_sum(grad_down_two),
    )


def solution(mesh):
    both = ("blk", "mp")
    return jax.shard_map(
        shards,
        mesh=mesh,
        in_specs=(
            P(("seqs", "blk"), None),
            P(("seqs", "blk"), None),
            P("seqs"),
            P("seqs"),
            P("seqs", None, both),
            P("seqs", None, both),
            P("seqs", None, "blk", "mp"),
            P(None, "blk"),
            P(None, None, both),
            P(None, both),
            P(both),
            P(None, both),
            P(None, both),
            P(both),
            P(None, both),
            P(both),
            P(both, None),
            P(None, None, both),
            P(both, None),
            P(None, "blk", "mp"),
            P("mp", "blk"),
            P(None, None, both),
            P(both, None),
        ),
        out_specs=(
            P(("seqs", "blk"), None),
            P(("seqs", "blk"), None),
            P("seqs", None, both),
            P("seqs", None, both),
            P("seqs", None, "blk", "mp"),
            P("seqs", None, both),
            P("seqs", None, both),
            P("seqs", None, "blk", "mp"),
            P(None, "blk"),
            P(None, None, both),
            P(None, both),
            P(both),
            P(None, both),
            P(None, both),
            P(both),
            P(None, both),
            P(both),
            P(both, None),
            P(None, None, both),
            P(both, None),
            P(None, "blk", "mp"),
            P("mp", "blk"),
            P(None, None, both),
            P(both, None),
        ),
        check_vma=False,
    )
```
